256 devices in a mesh: pipe: 8 (over x, core), vocab: 32 (over z, y).
Axes of the slice: x: 4, y: 4, z: 8, core: 2. Of those that a mesh axis runs over, the one named last changes fastest.
Arguments:
- hidden: bfloat16 [8, 128, 4096], P('pipe'), may hold values from -60 to 60
- norm_gain: float32 [4096], replicated, may hold values from 0.5 to 1.5
- out_weight: bfloat16 [128256, 4096], P(('pipe', 'vocab')), may hold values from -4 to 4
- targets: int32 [8, 128], P('pipe'), may hold values from 0 to 128255
- loss_mask: int32 [8, 128], P('pipe'), may hold values from 0 to 1, as said below
- slot_position: int32 [8, 128], P('pipe'), may hold values from 0 to 127, each once within a row
- counts: int32 [8], replicated, may hold values from 1 to 128, 640 in all
- loss_scale: float32 [], replicated, may hold values from 4096 to 32768
Outputs:
- loss: float32 [], replicated
- grad_hidden: bfloat16 [8, 128, 4096], P('pipe')
The draws below stay inside these ranges and needn't reach their ends.
Inputs may be any that keep to these rules, and one draw needn't show every extreme that they name: The 8 counts sum to exactly 640, and one of them equals 128. Each row of slot_position holds every number of 0 to 127 once. Each row of loss_mask holds at least 64 ones.
All inputs are finite; a program needn't handle non-finite values.
Results may differ from the reference program's by a relative error of at most 0.0034.
Values may be sent and summed in bfloat16 or wider, within the bound.
No kernel may reach another device: no remote copies, remote signals or barrier semaphores. Data moves between devices by JAX's collectives and lax.ppermute only.
A program may use at most 64 MiB of HBM per device.

```python
import math
import jax
import jax.numpy as jnp
import numpy as np
from jax import lax

D = 4096
VOCAB = 128256
TOK_MB = 128
MICRO = 8
LIVE = 640


def make_hidden(key):
    folded = jax.random.fold_in(key, 11)
    key_scale, key_noise = jax.random.split(folded)
    scales = jnp.exp(jax.random.uniform(key_scale, (MICRO, TOK_MB, 1), jnp.float32) * math.log(10.0))
    raw_noise = jnp.clip(jax.random.normal(key_noise, (MICRO, TOK_MB, D), jnp.float32), -6.0, 6.0)
    return raw_noise * scales


def draw_hidden(key, part):
    return make_hidden(key).astype(jnp.bfloat16)


def draw_out_weight(key, part):
    folded = jax.random.fold_in(key, 23)
    key_weight = jax.random.fold_in(folded, 0)
    weight = jnp.clip(jax.random.normal(key_weight, (VOCAB, D), jnp.float32), -6.0, 6.0) * (3.0 / math.sqrt(D))
    return weight.astype(jnp.bfloat16)


def draw_loss_mask(key, part):
    folded = jax.random.fold_in(key, 37)
    key_count, key_order = jax.random.split(folded)
    ones_count = jax.random.randint(key_count, (MICRO, 1), TOK_MB // 2, TOK_MB + 1)
    order_keys = jax.random.split(key_order, MICRO)
    ranks = jax.vmap(lambda one_key: jax.random.permutation(one_key, TOK_MB))(order_keys)
    return jnp.where(ranks < ones_count, 1, 0).astype(jnp.int32)


def place_ends(entries, rng, low, largest):
    longest = entries.shape.index(max(entries.shape))
    spots = []
    for shift in (0, 1):
        where = [jax.random.randint(jax.random.fold_in(rng, axis), (), 0, length) for axis, length in enumerate(entries.shape)]
        where[longest] = (where[longest] + shift) % entries.shape[longest]
        spots.append(tuple(where))
    return entries.at[spots[0]].set(low).at[spots[1]].set(largest)


def ranked_wide(own_key, shape, count, lean):
    weights = [min(1 << octave, count + 1 - (1 << octave)) * (1 << 20) // math.isqrt((1 << octave) ** lean) + 1 for octave in range((count + 1).bit_length()) if 1 << octave <= count]
    spread = 1 + sum(weights) // (1 << 30)
    table = np.cumsum(np.array([max(1, weight // spread) for weight in weights]))
    lot = jax.random.randint(jax.random.fold_in(own_key, 1), shape, 0, int(table[len(weights) - 1]))
    start = jnp.left_shift(1, jnp.searchsorted(jnp.asarray(table, jnp.int32), lot, side="right").astype(jnp.int32))
    standing = start - 1 + jax.random.randint(jax.random.fold_in(own_key, 4), shape, 0, 1 << 30) % jnp.minimum(start, count + 1 - start)
    return jax.random.permutation(jax.random.fold_in(own_key, 2), count)[standing].astype(jnp.int32)


def length_profile(amount, total, bound, skew):
    weights = [(1 << 20) // math.isqrt(rank ** skew) + 1 for rank in range(2, amount + 1)]
    spare, holding = total - bound - (amount - 1), [1] * (amount - 1)
    while spare > 0:
        movable = [i for i in range(amount - 1) if holding[i] < bound]
        whole, left = sum([weights[i] for i in movable]), spare
        for i in movable:
            addition = min(bound - holding[i], max(1, left * weights[i] // whole), spare)
            holding[i] = holding[i] + addition
            spare = spare - addition
    return np.array([bound] + holding)


def uneven_parts(own_key, number_of, total, reach, lean):
    if number_of == 2:
        one = jax.random.randint(own_key, (), max(1, total - reach), min(reach, total - 1) + 1)
        return jnp.stack([one, total - one])
    sizes = jnp.asarray(length_profile(number_of, total, reach, lean), jnp.int32)
    couples = (number_of - 1) // 2
    donor, sink = sizes[1:1 + 2 * couples:2], sizes[2:2 + 2 * couples:2]
    margin = jnp.minimum(donor - 1, reach - sink)
    shifted = jax.random.randint(jax.random.fold_in(own_key, 1), (couples,), 0, 1 << 20) % (margin + 1)
    sizes = sizes.at[1:1 + 2 * couples:2].set(donor - shifted).at[2:2 + 2 * couples:2].set(sink + shifted)
    return sizes[jax.random.permutation(jax.random.fold_in(own_key, 2), number_of)]


def setup_inputs(seed: int = 0) -> dict:
    seeds = jax.random.split(jax.random.key(seed), 9)
    return {
        "hidden": draw_hidden(jax.random.fold_in(seeds[8], 71), 0),
        "norm_gain": jnp.clip(1.0 + 0.1 * jax.random.normal(seeds[1], (D,), jnp.float32), 0.5, 1.5),
        "out_weight": draw_out_weight(jax.random.fold_in(seeds[8], 71), 0),
        "targets": place_ends(ranked_wide(seeds[3], (MICRO, TOK_MB), VOCAB, 2), jax.random.fold_in(seeds[3], 3), 0, VOCAB - 1).astype(jnp.int32),
        "loss_mask": draw_loss_mask(jax.random.fold_in(seeds[8], 71), 0),
        "slot_position": jax.vmap(lambda own: jax.random.permutation(own, TOK_MB))(jax.random.split(seeds[5], MICRO)).reshape((MICRO, TOK_MB)).astype(jnp.int32),
        "counts": uneven_parts(seeds[6], MICRO, LIVE, TOK_MB, 2).astype(jnp.int32),
        "loss_scale": jnp.clip(jnp.exp(jax.random.uniform(seeds[7], (), jnp.float32, math.log(4096.0), math.log(32768.0))), 4096.0, 32768.0),
    }


EPSILON = 1e-05

def rms_scale(values, norm_gain):
    mean_square = lax.optimization_barrier(jnp.mean(values * values, axis=-1, keepdims=True))
    return values * lax.rsqrt(mean_square + EPSILON) * norm_gain.astype(jnp.float32)

def micro_terms(normed_rows, target_row, weight_row, out_weight, loss_scale, weight_total):
    logits = lax.dot_general(normed_rows, out_weight, (((1,), (1,)), ((), ())), preferred_element_type=jnp.float32)
    row_top = lax.optimization_barrier(jnp.max(logits, axis=1))
    exp_total = lax.optimization_barrier(jnp.sum(jnp.exp(logits - row_top[:, None]), axis=1))
    log_total = row_top + jnp.log(exp_total)
    is_target = jnp.arange(VOCAB, dtype=jnp.int32)[None, :] == target_row.astype(jnp.int32)[:, None]
    target_logit = lax.optimization_barrier(jnp.sum(jnp.where(is_target, logits, 0.0), axis=1))
    loss_part = jnp.sum(weight_row * (log_total - target_logit))
    token_coef = loss_scale * weight_row / weight_total
    logit_grad = ((jnp.exp(logits - log_total[:, None]) - is_target.astype(jnp.float32)) * token_coef[:, None]).astype(jnp.bfloat16)
    normed_grad = jnp.dot(logit_grad, out_weight, preferred_element_type=jnp.float32)
    return (loss_part, normed_grad)

def reference(hidden, norm_gain, out_weight, targets, loss_mask, slot_position, counts, loss_scale):
    rows_total = MICRO * TOK_MB
    flat = hidden.reshape(rows_total, D).astype(jnp.float32)
    normed = rms_scale(flat, norm_gain).astype(jnp.bfloat16)
    inside = slot_position < counts[:, None]
    token_weight = jnp.where(inside & (loss_mask == 1), 1.0, 0.0).astype(jnp.float32)
    weight_total = jnp.sum(token_weight)

    def one_micro(item):
        return micro_terms(item[0], item[1], item[2], out_weight, loss_scale, weight_total)
    loss_parts, normed_grad = lax.map(one_micro, (normed.reshape(MICRO, TOK_MB, D), targets, token_weight))
    loss = jnp.sum(loss_parts) / weight_total
    pullback = jax.vjp(lambda values: rms_scale(values, norm_gain), flat)[1]
    grad_flat = pullback(normed_grad.reshape(rows_total, D))[0]
    return (loss, grad_flat.astype(jnp.bfloat16).reshape(MICRO, TOK_MB, D))
```

```python
import jax
import jax.numpy as jnp
from jax import lax
from jax.sharding import Mesh
from jax.sharding import PartitionSpec as P

AXES = ("x", "c", "z", "y")
SIZE = {"x": 4, "c": 2, "z": 8, "y": 4}
PIPE = ("x", "c")
LIVE = 640
EPSILON = 1e-05
BF16, F16, F32 = jnp.bfloat16, jnp.float16, jnp.float32


def shift(value, axis, by):
    n = SIZE[axis]
    return lax.ppermute(value, axis, [(i, (i + by) % n) for i in range(n)])


def swap_cores(value):
    return lax.ppermute(value, "c", [(0, 1), (1, 0)])


def place(pieces, axis):
    own = lax.axis_index(axis)
    out = jnp.zeros((4,) + pieces[0].shape, pieces[0].dtype)
    for k, piece in enumerate(pieces):
        out = lax.dynamic_update_index_in_dim(out, piece, (own + k) % 4, 0)
    return out


def gather_direct(chunk, axis):
    return [chunk, shift(chunk, axis, -1), shift(chunk, axis, 2), shift(chunk, axis, 1)]


def gather_ring(chunk, axis):
    half = chunk.shape[0] // 2
    below, above = shift(chunk, axis, 1), shift(chunk, axis, -1)
    first, second = shift(below[:half], axis, 1), shift(above[half:], axis, -1)
    return [chunk, above, jnp.concatenate([first, second], 0), below]


def pick(chunks, axis, k):
    own = lax.axis_index(axis)
    return lax.dynamic_index_in_dim(chunks, (own + k) % 4, 0, keepdims=False)


def scatter_direct(chunks, axis):
    got = [shift(pick(chunks, axis, k).astype(F16), axis, k) for k in (1, 2, 3)]
    total = pick(chunks, axis, 0)
    for g in got:
        total = total + g.astype(F32)
    return total


def scatter_ring(chunks, axis):
    half = chunks.shape[1] // 2
    far = pick(chunks, axis, 2).astype(F16)
    first, second = shift(far[:half], axis, 1), shift(far[half:], axis, -1)
    up, down = pick(chunks, axis, 1), pick(chunks, axis, 3)
    up = jnp.concatenate([up[:half] + first.astype(F32), up[half:]], 0).astype(F16)
    down = jnp.concatenate([down[:half], down[half:] + second.astype(F32)], 0).astype(F16)
    got_below, got_above = shift(up, axis, 1), shift(down, axis, -1)
    return pick(chunks, axis, 0) + got_below.astype(F32) + got_above.astype(F32)


def exchange(value, axes):
    return lax.all_to_all(value, axes, 0, 0)


def everyone(value, axes):
    n = 1
    for a in axes:
        n *= SIZE[a]
    return exchange(jnp.broadcast_to(value[None], (n,) + value.shape), axes)


def merge(stats):
    top = jnp.max(stats[:, 0], axis=0)
    total = jnp.sum(stats[:, 1] * jnp.exp(stats[:, 0] - top[None]), axis=0)
    return jnp.stack([top, total, jnp.sum(stats[:, 2], axis=0)])


def body(hidden, norm_gain, out_weight, targets, loss_mask, slot_position, counts, loss_scale):
    slots, width = hidden.shape[1], hidden.shape[2]
    words = out_weight.shape[0]
    core, y = lax.axis_index("c"), lax.axis_index("y")
    offset = lax.axis_index(AXES) * words
    half = width // 2
    mine = lax.dynamic_slice_in_dim(out_weight, core * half, half, 1)
    sent = lax.dynamic_slice_in_dim(out_weight, (1 - core) * half, half, 1)
    other = swap_cores(sent)

    rows = hidden.reshape(slots, width).astype(F32)
    scale = lax.rsqrt(jnp.mean(rows * rows, axis=-1, keepdims=True) + EPSILON)
    normed = (rows * scale * norm_gain).astype(BF16)

    parts = normed.T.reshape(2, 2, 4, 4, 64, slots)
    first = lax.dynamic_index_in_dim(parts[:, 0], y, 2, keepdims=False)
    second = lax.dynamic_index_in_dim(parts[:, 1], y, 1, keepdims=False)
    slices = jnp.stack([first, second], 2).transpose(1, 0, 2, 3, 4).reshape(8, 128, slots)
    t = targets.reshape(1, slots)
    info = jnp.concatenate(
        [t & 255, (t >> 8) & 255, t >> 16, loss_mask.reshape(1, slots), slot_position.reshape(1, slots)]
        + [jnp.zeros((11, slots), jnp.int32)],
        0,
    ).astype(BF16)
    packed = jnp.concatenate([slices, jnp.broadcast_to(info[None], (8, 16, slots))], 1)
    packed = exchange(packed, PIPE)

    mask, position = packed[:, 131].astype(F32), packed[:, 132].astype(F32)
    live = (position < counts.astype(F32)[:, None]) & (mask == 1)
    live_f = live.astype(F32)
    before = jnp.dot(
        live_f.astype(BF16),
        (jnp.arange(slots)[:, None] < jnp.arange(slots)[None, :]).astype(BF16),
        preferred_element_type=F32,
    )
    per_micro = jnp.sum(live_f, axis=1)
    base = jnp.sum(jnp.where(jnp.arange(8)[:, None] > jnp.arange(8)[None, :], per_micro[None, :], 0.0), axis=1)
    weight_total = jnp.sum(per_micro)
    column = jnp.where(live, before + base[:, None], -1.0).reshape(8 * slots)
    select = column[:, None] == jnp.arange(LIVE, dtype=F32)[None, :]
    wide = packed.transpose(1, 0, 2).reshape(144, 8 * slots)
    compact = jnp.dot(wide, select.astype(BF16), preferred_element_type=F32)
    digits = compact[128:131].astype(jnp.int32)
    work_targets = digits[0] + (digits[1] << 8) + (digits[2] << 16)
    compact = compact[:128].astype(BF16)

    near_one = place(gather_direct(compact[:64], "y"), "y").reshape(256, LIVE)
    near_two = place(gather_direct(compact[64:], "x"), "x").reshape(256, LIVE)
    one = place(gather_ring(near_one, "x"), "x").reshape(1024, LIVE)
    two = place(gather_ring(near_two, "y"), "y").reshape(1024, LIVE)
    states = jnp.concatenate([one, two], 0)

    sib = jnp.dot(other, states, preferred_element_type=F32)
    logits = jnp.dot(mine, states, preferred_element_type=F32) + swap_cores(sib)

    is_target = jnp.arange(words, dtype=jnp.int32)[:, None] == (work_targets - offset)[None, :]
    top = jnp.max(logits, axis=0)
    stats = jnp.stack(
        [top, jnp.sum(jnp.exp(logits - top[None]), axis=0), jnp.sum(jnp.where(is_target, logits, 0.0), axis=0)]
    )
    stats = merge(jnp.stack([stats, swap_cores(stats)]))
    stats = merge(everyone(stats, ("x", "y")))
    stats = merge(everyone(stats, ("z",)))
    log_total = stats[0] + jnp.log(stats[1])
    weight = (jnp.arange(LIVE, dtype=F32) < weight_total).astype(F32)
    loss = jnp.sum(weight * (log_total - stats[2])) / weight_total
    coef = loss_scale * weight / weight_total
    logit_grad = (
        (jnp.exp(logits - log_total[None]) - is_target.astype(F32)) * coef[None]
    ).astype(BF16)
    other_grad = swap_cores(logit_grad)
    dims = (((0,), (0,)), ((), ()))
    grad = lax.dot_general(mine, logit_grad, dims, preferred_element_type=F32) + lax.dot_general(
        other, other_grad, dims, preferred_element_type=F32
    )

    one = scatter_ring(grad[:1024].reshape(4, 256, LIVE), "x")
    two = scatter_ring(grad[1024:].reshape(4, 256, LIVE), "y")
    one = scatter_direct(one.reshape(4, 64, LIVE), "y")
    two = scatter_direct(two.reshape(4, 64, LIVE), "x")
    chunk = jnp.concatenate([one.reshape(8, 8, LIVE), two.reshape(8, 8, LIVE)], 1).astype(F16)
    chunk = jnp.sum(exchange(chunk, ("z",)).astype(F32), axis=0)
    spread = lax.dot_general(
        chunk, select.astype(F32), (((1,), (1,)), ((), ())), precision=lax.Precision.HIGHEST,
        preferred_element_type=F32,
    )
    spread = spread.reshape(16, 8, slots).transpose(1, 0, 2).astype(F16)
    spread = exchange(spread, PIPE).reshape(128, slots)
    full = everyone(spread, ("z", "y"))
    full = full.reshape(8, 4, 4, 2, 2, 8, slots)
    one = full[:, :, :, :, 0].transpose(3, 2, 1, 0, 4, 5).reshape(2, 1, 1024, slots)
    two = full[:, :, :, :, 1].transpose(3, 1, 2, 0, 4, 5).reshape(2, 1, 1024, slots)
    normed_grad = jnp.concatenate([one, two], 1).reshape(width, slots).T.astype(F32)

    pulled = normed_grad * norm_gain
    inner = jnp.sum(rows * pulled, axis=-1, keepdims=True) / width
    out = scale * pulled - scale * scale * scale * rows * inner
    return loss, out.astype(BF16).reshape(1, slots, width)


def solution(mesh):
    split = Mesh(mesh.devices.reshape(4, 2, 8, 4), AXES)
    return jax.shard_map(
        body,
        mesh=split,
        in_specs=(
            P(PIPE, None, None),
            P(),
            P(AXES, None),
            P(PIPE, None),
            P(PIPE, None),
            P(PIPE, None),
            P(),
            P(),
        ),
        out_specs=(P(), P(PIPE, None, None)),
        check_vma=False,
    )
```

```python
import jax
import jax.numpy as jnp
from jax import lax
from jax.experimental import pallas as pl
from jax.experimental.pallas import tpu as pltpu
from jax.sharding import Mesh
from jax.sharding import PartitionSpec as P

AXES = ("x", "c", "z", "y")
SIZE = {"x": 4, "c": 2, "z": 8, "y": 4}
PIPE = ("x", "c")
LIVE = 640
EPSILON = 1e-05
BF16, F16, F32 = jnp.bfloat16, jnp.float16, jnp.float32


def shift(value, axis, by):
    n = SIZE[axis]
    return lax.ppermute(value, axis, [(i, (i + by) % n) for i in range(n)])


def swap_cores(value):
    return lax.ppermute(value, "c", [(0, 1), (1, 0)])


def place(pieces, axis):
    own = lax.axis_index(axis)
    out = jnp.zeros((4,) + pieces[0].shape, pieces[0].dtype)
    for k, piece in enumerate(pieces):
        out = lax.dynamic_update_index_in_dim(out, piece, (own + k) % 4, 0)
    return out


def gather_direct(chunk, axis):
    return [chunk, shift(chunk, axis, -1), shift(chunk, axis, 2), shift(chunk, axis, 1)]


def gather_ring(chunk, axis):
    half = chunk.shape[0] // 2
    below, above = shift(chunk, axis, 1), shift(chunk, axis, -1)
    first, second = shift(below[:half], axis, 1), shift(above[half:], axis, -1)
    return [chunk, above, jnp.concatenate([first, second], 0), below]


def pick(chunks, axis, k):
    own = lax.axis_index(axis)
    return lax.dynamic_index_in_dim(chunks, (own + k) % 4, 0, keepdims=False)


def scatter_direct(chunks, axis):
    got = [shift(pick(chunks, axis, k).astype(F16), axis, k) for k in (1, 2, 3)]
    total = pick(chunks, axis, 0)
    for g in got:
        total = total + g.astype(F32)
    return total


def scatter_ring(chunks, axis):
    half = chunks.shape[1] // 2
    far = pick(chunks, axis, 2).astype(F16)
    first, second = shift(far[:half], axis, 1), shift(far[half:], axis, -1)
    up, down = pick(chunks, axis, 1), pick(chunks, axis, 3)
    up = jnp.concatenate([up[:half] + first.astype(F32), up[half:]], 0).astype(F16)
    down = jnp.concatenate([down[:half], down[half:] + second.astype(F32)], 0).astype(F16)
    got_below, got_above = shift(up, axis, 1), shift(down, axis, -1)
    return pick(chunks, axis, 0) + got_below.astype(F32) + got_above.astype(F32)


def exchange(value, axes):
    return lax.all_to_all(value, axes, 0, 0)


def everyone(value, axes):
    n = 1
    for a in axes:
        n *= SIZE[a]
    return exchange(jnp.broadcast_to(value[None], (n,) + value.shape), axes)


def merge(stats):
    top = jnp.max(stats[:, 0], axis=0)
    total = jnp.sum(stats[:, 1] * jnp.exp(stats[:, 0] - top[None]), axis=0)
    return jnp.stack([top, total, jnp.sum(stats[:, 2], axis=0)])


NT = (((1,), (1,)), ((), ()))
TN = (((0,), (0,)), ((), ()))
MIB = 1024 * 1024
VM, SM = pl.BlockSpec(memory_space=pltpu.VMEM), pl.BlockSpec(memory_space=pltpu.SMEM)


def slice_kernel(y_ref, h_ref, gain_ref, target_ref, mask_ref, position_ref, out_ref, scales, turned):
    slots, width = h_ref.shape
    half, quarter = width // 2, width // 4

    def step(i, carry):
        at = pl.ds(pl.multiple_of(i * 16, 16), 16)
        values = h_ref[at, :].astype(F32)
        mean = jnp.sum(values * values, axis=1, keepdims=True) / width
        scales[at, :] = jnp.broadcast_to(lax.rsqrt(mean + EPSILON), (16, 128))
        return carry

    lax.fori_loop(0, slots // 16, step, 0)
    y = y_ref[0]

    def tile(offset):
        at = pl.ds(pl.multiple_of(offset, 128), 128)
        return (h_ref[:, at].astype(F32) * scales[...] * gain_ref[:, at]).T

    word = target_ref[...]
    rows = [word & 255, (word >> 8) & 255, word >> 16, mask_ref[...], position_ref[...]]
    info = jnp.concatenate(rows + [jnp.zeros_like(word)] * 11, 0).astype(F32).astype(BF16)
    for core in range(2):
        for x in range(4):
            turned[x] = tile(core * half + x * 256 + (y // 2) * 128)
        for x in range(4):
            to = x * 2 + core
            out_ref[to, 0:64, :] = turned[x, pl.ds(pl.multiple_of((y % 2) * 64, 64), 64), :].astype(BF16)
            out_ref[to, 128:144, :] = info
        for pair in range(2):
            both = tile(core * half + quarter + y * 256 + pair * 128).astype(BF16)
            out_ref[4 * pair + core, 64:128, :] = both[:64]
            out_ref[4 * pair + 2 + core, 64:128, :] = both[64:]


def slices_of(y, rows, gain, targets, mask, position):
    slots, width = rows.shape
    return pl.pallas_call(
        slice_kernel,
        name="normed_slices",
        out_shape=jax.ShapeDtypeStruct((8, 144, slots), BF16),
        in_specs=[SM] + [VM] * 5,
        out_specs=VM,
        scratch_shapes=[pltpu.VMEM((slots, 128), F32), pltpu.VMEM((4, 128, slots), F32)],
        cost_estimate=pl.CostEstimate(flops=4 * slots * width, bytes_accessed=4 * slots * width, transcendentals=slots),
    )(y, rows, gain.reshape(1, width), targets, mask, position)


def stats_kernel(count_ref, own_ref, other_ref, word_ref, logit_ref, stat_ref):
    words = own_ref.shape[0]
    total = jnp.zeros((1, 128), F32)
    for t in range(LIVE // 128):
        at = slice(t * 128, t * 128 + 128)
        logits = own_ref[:, at] + other_ref[:, at]
        logit_ref[:, at] = logits
        top = jnp.max(logits, axis=0, keepdims=True)
        stat_ref[t : t + 1, :] = top + jnp.log(jnp.sum(jnp.exp(logits - top), axis=0, keepdims=True))
        hit = lax.broadcasted_iota(jnp.int32, (words, 128), 0) == word_ref[:, at]
        chosen = jnp.sum(jnp.where(hit, logits, 0.0), axis=0, keepdims=True)
        spot = lax.broadcasted_iota(jnp.int32, (1, 128), 1) + t * 128
        total = total + jnp.where(spot.astype(F32) < count_ref[0], chosen, 0.0)
    stat_ref[5:8, :] = jnp.broadcast_to(jnp.sum(total, axis=1, keepdims=True), (3, 128))


def stats_of(count, own, other, word):
    words = own.shape[0]
    return pl.pallas_call(
        stats_kernel,
        name="stats",
        out_shape=(jax.ShapeDtypeStruct((words, LIVE), F32), jax.ShapeDtypeStruct((8, 128), F32)),
        in_specs=[SM] + [VM] * 3,
        out_specs=(VM, VM),
        cost_estimate=pl.CostEstimate(flops=8 * words * LIVE, bytes_accessed=12 * words * LIVE, transcendentals=words * LIVE),
    )(count, own, other, word)


def grad_kernel(logit_ref, total_ref, coef_ref, word_ref, out_ref):
    words = logit_ref.shape[0]
    for t in range(LIVE // 128):
        at = slice(t * 128, t * 128 + 128)
        hit = lax.broadcasted_iota(jnp.int32, (words, 128), 0) == word_ref[:, at]
        value = (jnp.exp(logit_ref[:, at] - total_ref[t : t + 1, :]) - hit.astype(F32)) * coef_ref[t : t + 1, :]
        out_ref[:, at] = value.astype(BF16)


def grad_of(logits, total, coef, word):
    words = logits.shape[0]
    return pl.pallas_call(
        grad_kernel,
        name="logit_grad",
        out_shape=jax.ShapeDtypeStruct((words, LIVE), BF16),
        in_specs=[VM] * 4,
        out_specs=VM,
        cost_estimate=pl.CostEstimate(flops=4 * words * LIVE, bytes_accessed=6 * words * LIVE, transcendentals=words * LIVE),
    )(logits, total, coef, word)


def finish_kernel(grad_ref, h_ref, gain_ref, out_ref, turned):
    slots, width = h_ref.shape
    for core in range(2):
        for part in range(2):
            for a in range(4):
                for b in range(2):
                    blocks = []
                    for pair in range(2):
                        for z in range(8):
                            other = 2 * b + pair
                            y, x = (other, a) if part == 0 else (a, other)
                            blocks.append(grad_ref[y, z, x, core, part])
                    at = core * (width // 2) + part * (width // 4) + a * 256 + b * 128
                    turned[:, at : at + 128] = jnp.concatenate(blocks, 0).T

    def step(i, carry):
        at = pl.ds(pl.multiple_of(i * 16, 16), 16)
        values = h_ref[at, :].astype(F32)
        scale = lax.rsqrt(jnp.sum(values * values, axis=1, keepdims=True) / width + EPSILON)
        pulled = turned[at, :] * gain_ref[...]
        inner = jnp.sum(values * pulled, axis=1, keepdims=True) / width
        out_ref[at, :] = (scale * pulled - scale * scale * scale * values * inner).astype(BF16)
        return carry

    lax.fori_loop(0, slots // 16, step, 0)


def finish(grad, rows, gain):
    slots, width = rows.shape
    vmem = pl.BlockSpec(memory_space=pltpu.VMEM)
    return pl.pallas_call(
        finish_kernel,
        out_shape=jax.ShapeDtypeStruct((slots, width), BF16),
        in_specs=[vmem] * 3,
        out_specs=vmem,
        scratch_shapes=[pltpu.VMEM((slots, width), F32)],
        compiler_params=pltpu.CompilerParams(vmem_limit_bytes=16 * MIB),
        cost_estimate=pl.CostEstimate(flops=8 * slots * width, bytes_accessed=8 * slots * width, transcendentals=slots),
    )(grad, rows, gain.reshape(1, width))


def merge_rows(rows):
    top = jnp.max(rows, axis=0)
    joined = top + jnp.log(jnp.sum(jnp.exp(rows - top[None]), axis=0))
    return jnp.where(jnp.arange(8)[:, None] < 5, joined, jnp.sum(rows, axis=0))


def body(hidden, norm_gain, out_weight, targets, loss_mask, slot_position, counts, loss_scale):
    slots, width = hidden.shape[1], hidden.shape[2]
    words = out_weight.shape[0]
    core, y = lax.axis_index("c"), lax.axis_index("y")
    offset = lax.axis_index(AXES) * words
    half = width // 2
    raw = hidden.reshape(slots, width)
    packed = slices_of(y.reshape(1).astype(jnp.int32), raw, norm_gain, targets, loss_mask, slot_position)
    packed, late_weight = lax.optimization_barrier((packed, out_weight))
    packed = exchange(packed, PIPE)
    mine = lax.dynamic_slice_in_dim(late_weight, core * half, half, 1)
    other = swap_cores(lax.dynamic_slice_in_dim(late_weight, (1 - core) * half, half, 1))

    mask, position = packed[:, 131].astype(F32), packed[:, 132].astype(F32)
    live = (position < counts.astype(F32)[:, None]) & (mask == 1)
    live_f = live.astype(F32)
    before = jnp.dot(
        live_f.astype(BF16),
        (jnp.arange(slots)[:, None] < jnp.arange(slots)[None, :]).astype(BF16),
        preferred_element_type=F32,
    )
    per_micro = jnp.sum(live_f, axis=1)
    base = jnp.sum(jnp.where(jnp.arange(8)[:, None] > jnp.arange(8)[None, :], per_micro[None, :], 0.0), axis=1)
    weight_total = jnp.sum(per_micro)
    column = jnp.where(live, before + base[:, None], -1.0).reshape(8 * slots)
    select = column[:, None] == jnp.arange(LIVE, dtype=F32)[None, :]
    wide = packed.transpose(1, 0, 2).reshape(144, 8 * slots)
    compact = jnp.dot(wide, select.astype(BF16), preferred_element_type=F32)
    digits = compact[128:131].astype(jnp.int32)
    word = (digits[0] + (digits[1] << 8) + (digits[2] << 16) - offset).reshape(1, LIVE)
    compact = compact[:128].astype(BF16)

    near_one = place(gather_direct(compact[:64], "y"), "y").reshape(256, LIVE)
    near_two = place(gather_direct(compact[64:], "x"), "x").reshape(256, LIVE)
    one = place(gather_ring(near_one, "x"), "x").reshape(1024, LIVE)
    two = place(gather_ring(near_two, "y"), "y").reshape(1024, LIVE)
    states = jnp.concatenate([one, two], 0)

    sib = jnp.dot(other, states, preferred_element_type=F32)
    sib, states = lax.optimization_barrier((sib, states))
    own = jnp.dot(mine, states, preferred_element_type=F32)
    logits, stats = stats_of(weight_total.reshape(1), own, swap_cores(sib), word)
    stats = merge_rows(everyone(stats, ("z", "y")))
    stats = merge_rows(everyone(stats, PIPE))
    weight = (jnp.arange(8 * slots, dtype=F32).reshape(8, slots) < weight_total).astype(F32)
    loss = (jnp.sum((weight * stats)[:5]) - stats[5, 0]) / weight_total
    coef = loss_scale * weight / weight_total
    logit_grad = grad_of(logits, stats, coef, word)
    other_grad = swap_cores(logit_grad)
    grad = lax.dot_general(mine, logit_grad, TN, preferred_element_type=F32) + lax.dot_general(
        other, other_grad, TN, preferred_element_type=F32
    )

    one = scatter_ring(grad[:1024].reshape(4, 256, LIVE), "x")
    two = scatter_ring(grad[1024:].reshape(4, 256, LIVE), "y")
    one = scatter_direct(one.reshape(4, 64, LIVE), "y")
    two = scatter_direct(two.reshape(4, 64, LIVE), "x")
    chunk = jnp.concatenate([one.reshape(8, 8, LIVE), two.reshape(8, 8, LIVE)], 1).reshape(128, LIVE)
    spread = lax.dot_general(
        chunk, select.astype(F32), NT, precision=lax.Precision.HIGHEST, preferred_element_type=F32
    )
    spread = spread.astype(F16).reshape(8, 16, 8, slots).transpose(2, 0, 1, 3).reshape(64, 16, slots)
    spread = exchange(spread, ("x", "c", "z")).reshape(8, 8, 16, slots)
    spread = jnp.sum(spread.astype(F32), axis=1).astype(F16).reshape(128, slots)
    full = everyone(spread, ("z",)).reshape(1024, slots)
    full = place(gather_ring(full, "y"), "y").astype(F32).reshape(4, 8, 4, 2, 2, 8, slots)
    return loss, finish(full, raw, norm_gain).reshape(1, slots, width)


def solution(mesh):
    split = Mesh(mesh.devices.reshape(4, 2, 8, 4), AXES)
    return jax.shard_map(
        body,
        mesh=split,
        in_specs=(
            P(PIPE, None, None),
            P(),
            P(AXES, None),
            P(PIPE, None),
            P(PIPE, None),
            P(PIPE, None),
            P(),
            P(),
        ),
        out_specs=(P(), P(PIPE, None, None)),
        check_vma=False,
    )
```

```python
import jax
import jax.numpy as jnp
from jax import lax
from jax.experimental import pallas as pl
from jax.experimental.pallas import tpu as pltpu
from jax.sharding import Mesh
from jax.sharding import PartitionSpec as P

AXES = ("x", "c", "z", "y")
SIZE = {"x": 4, "c": 2, "z": 8, "y": 4}
PIPE = ("x", "c")
LIVE = 640
EPSILON = 1e-05
BF16, F16, F32 = jnp.bfloat16, jnp.float16, jnp.float32


def shift(value, axis, by):
    n = SIZE[axis]
    return lax.ppermute(value, axis, [(i, (i + by) % n) for i in range(n)])


def swap_cores(value):
    return lax.ppermute(value, "c", [(0, 1), (1, 0)])


def place(pieces, axis):
    own = lax.axis_index(axis)
    out = jnp.zeros((4,) + pieces[0].shape, pieces[0].dtype)
    for k, piece in enumerate(pieces):
        out = lax.dynamic_update_index_in_dim(out, piece, (own + k) % 4, 0)
    return out


def gather_ring(chunk, axis):
    half = chunk.shape[0] // 2
    below, above = shift(chunk, axis, 1), shift(chunk, axis, -1)
    first, second = shift(below[:half], axis, 1), shift(above[half:], axis, -1)
    return [chunk, above, jnp.concatenate([first, second], 0), below]


def pick(chunks, axis, k):
    own = lax.axis_index(axis)
    return lax.dynamic_index_in_dim(chunks, (own + k) % 4, 0, keepdims=False)


def scatter_direct(chunks, axis):
    got = [shift(pick(chunks, axis, k).astype(F16), axis, k) for k in (1, 2, 3)]
    total = pick(chunks, axis, 0)
    for g in got:
        total = total + g.astype(F32)
    return total


def scatter_ring(chunks, axis):
    half = chunks.shape[1] // 2
    far = pick(chunks, axis, 2).astype(F16)
    first, second = shift(far[:half], axis, 1), shift(far[half:], axis, -1)
    up, down = pick(chunks, axis, 1), pick(chunks, axis, 3)
    up = jnp.concatenate([up[:half] + first.astype(F32), up[half:]], 0).astype(F16)
    down = jnp.concatenate([down[:half], down[half:] + second.astype(F32)], 0).astype(F16)
    got_below, got_above = shift(up, axis, 1), shift(down, axis, -1)
    return pick(chunks, axis, 0) + got_below.astype(F32) + got_above.astype(F32)


def exchange(value, axes):
    return lax.all_to_all(value, axes, 0, 0)


def everyone(value, axes):
    n = 1
    for a in axes:
        n *= SIZE[a]
    return exchange(jnp.broadcast_to(value[None], (n,) + value.shape), axes)


def merge(stats):
    top = jnp.max(stats[:, 0], axis=0)
    total = jnp.sum(stats[:, 1] * jnp.exp(stats[:, 0] - top[None]), axis=0)
    return jnp.stack([top, total, jnp.sum(stats[:, 2], axis=0)])


NT = (((1,), (1,)), ((), ()))
TN = (((0,), (0,)), ((), ()))
MIB = 1024 * 1024
VM, SM = pl.BlockSpec(memory_space=pltpu.VMEM), pl.BlockSpec(memory_space=pltpu.SMEM)


def slice_kernel(y_ref, h_ref, gain_ref, target_ref, mask_ref, position_ref, out_ref, scales):
    slots, width = h_ref.shape
    half, quarter = width // 2, width // 4

    def step(i, carry):
        at = pl.ds(pl.multiple_of(i * 16, 16), 16)
        values = h_ref[at, :].astype(F32)
        mean = jnp.sum(values * values, axis=1, keepdims=True) / width
        scales[at, :] = jnp.broadcast_to(lax.rsqrt(mean + EPSILON), (16, 128))
        return carry

    lax.fori_loop(0, slots // 16, step, 0)

    def tile(offset):
        at = pl.ds(pl.multiple_of(offset, 128), 128)
        return (h_ref[:, at].astype(F32) * scales[...] * gain_ref[:, at]).T.astype(BF16)

    word = target_ref[...]
    rows = [word & 255, (word >> 8) & 255, word >> 16, mask_ref[...], position_ref[...]]
    info = jnp.concatenate(rows + [jnp.zeros_like(word)] * 11, 0).astype(F32).astype(BF16)

    def fill(core, carry):
        for part in range(2):
            for x in range(4):
                out_ref[x * 2 + core, part * 128 : part * 128 + 128, :] = tile(core * half + x * 256 + part * 128)
                out_ref[x * 2 + core, 512:528, :] = info
            second = tile(core * half + quarter + y_ref[0] * 256 + part * 128)
            for x in range(4):
                out_ref[x * 2 + core, 256 + part * 128 : 384 + part * 128, :] = second
        return carry

    lax.fori_loop(0, 2, fill, 0)


def slices_of(y, rows, gain, targets, mask, position):
    slots, width = rows.shape
    return pl.pallas_call(
        slice_kernel,
        name="normed_slices",
        out_shape=jax.ShapeDtypeStruct((8, 528, slots), BF16),
        in_specs=[SM] + [VM] * 5,
        out_specs=VM,
        scratch_shapes=[pltpu.VMEM((slots, 128), F32)],
        cost_estimate=pl.CostEstimate(flops=4 * slots * width, bytes_accessed=4 * slots * width, transcendentals=slots),
    )(y, rows, gain.reshape(1, width), targets, mask, position)


def compact_kernel(offset_ref, loss_scale_ref, counts_ref, packed_ref, one_ref, two_ref, word_ref, column_ref, coef_ref, count_ref, acc):
    iota = lambda shape, axis: lax.broadcasted_iota(jnp.int32, shape, axis)
    rows = []
    for micro in range(8):
        codes = packed_ref[micro, 512:528, :].astype(F32)
        rows.append(((codes[4:5] < counts_ref[micro].astype(F32)) & (codes[3:4] == 1.0)).astype(F32))
    live = jnp.concatenate(rows, 0)
    before = jnp.dot(
        live.astype(BF16),
        jnp.where(iota((128, 128), 0) < iota((128, 128), 1), 1.0, 0.0).astype(BF16),
        preferred_element_type=F32,
    )
    per_micro = jnp.sum(live, axis=1, keepdims=True)
    base = [jnp.zeros((1, 1), F32)]
    for micro in range(8):
        base.append(base[-1] + per_micro[micro : micro + 1])
    count = base.pop()
    column = jnp.where(live > 0.0, before + jnp.concatenate(base, 0), -1.0).astype(jnp.int32)
    column_ref[...] = column
    spot = iota((8, 128), 0) * 128 + iota((8, 128), 1)
    coef_ref[...] = jnp.where(spot.astype(F32) < count, loss_scale_ref[0] / count, 0.0)
    count_ref[...] = jnp.broadcast_to(count, (8, 128))
    for n in range(4):
        values = jnp.concatenate([packed_ref[2 * n], packed_ref[2 * n + 1]], 1)
        places = [
            jnp.where(iota((LIVE, 128), 0) == column[m : m + 1], 1.0, 0.0).astype(BF16) for m in (2 * n, 2 * n + 1)
        ]
        part = lax.dot_general(values, jnp.concatenate(places, 1), NT, preferred_element_type=F32)
        acc[...] = part if n == 0 else acc[...] + part
    one_ref[...] = acc[0:256, :].astype(BF16)
    two_ref[...] = acc[256:512, :].astype(BF16)
    word = acc[512:513, :] + 256.0 * acc[513:514, :] + 65536.0 * acc[514:515, :]
    word_ref[...] = word.astype(jnp.int32) - offset_ref[0]


def compact_of(offset, loss_scale, counts, packed):
    tile, whole = jax.ShapeDtypeStruct((8, 128), F32), jax.ShapeDtypeStruct((8, 128), jnp.int32)
    wide = jax.ShapeDtypeStruct((256, LIVE), BF16)
    return pl.pallas_call(
        compact_kernel,
        name="compact",
        out_shape=(wide, wide, jax.ShapeDtypeStruct((1, LIVE), jnp.int32), whole, tile, tile),
        in_specs=[SM, SM, SM, VM],
        out_specs=(VM,) * 6,
        scratch_shapes=[pltpu.VMEM((528, LIVE), F32)],
        compiler_params=pltpu.CompilerParams(vmem_limit_bytes=12 * MIB),
        cost_estimate=pl.CostEstimate(flops=2 * 528 * 1024 * LIVE, bytes_accessed=3 * MIB, transcendentals=0),
    )(offset, loss_scale, counts, packed)


def product_kernel(weight_ref, one_ref, two_ref, out_ref):
    width = one_ref.shape[0]
    for at in (slice(0, 256), slice(256, 512), slice(512, 640)):
        out_ref[:, at] = jnp.dot(weight_ref[:, :width], one_ref[:, at], preferred_element_type=F32) + jnp.dot(
            weight_ref[:, width:], two_ref[:, at], preferred_element_type=F32
        )


def product(weight, one, two):
    words, width = weight.shape
    return pl.pallas_call(
        product_kernel,
        name="product",
        out_shape=jax.ShapeDtypeStruct((words, LIVE), F32),
        in_specs=[VM] * 3,
        out_specs=VM,
        compiler_params=pltpu.CompilerParams(vmem_limit_bytes=10 * MIB),
        cost_estimate=pl.CostEstimate(flops=2 * words * width * LIVE, bytes_accessed=6 * MIB, transcendentals=0),
    )(weight, one, two)


def pull_kernel(mine_ref, other_ref, grad_ref, other_grad_ref, out_ref):
    def step(i, carry):
        at = pl.ds(pl.multiple_of(i * 256, 256), 256)
        out_ref[at, :] = lax.dot_general(
            mine_ref[:, at], grad_ref[...], TN, preferred_element_type=F32
        ) + lax.dot_general(other_ref[:, at], other_grad_ref[...], TN, preferred_element_type=F32)
        return carry

    lax.fori_loop(0, out_ref.shape[0] // 256, step, 0)


def pull(mine, other, grad, other_grad):
    words, width = mine.shape
    return pl.pallas_call(
        pull_kernel,
        name="pull",
        out_shape=jax.ShapeDtypeStruct((width, LIVE), F32),
        in_specs=[VM] * 4,
        out_specs=VM,
        compiler_params=pltpu.CompilerParams(vmem_limit_bytes=14 * MIB),
        cost_estimate=pl.CostEstimate(flops=4 * words * width * LIVE, bytes_accessed=12 * MIB, transcendentals=0),
    )(mine, other, grad, other_grad)


def stats_kernel(count_ref, own_ref, other_ref, word_ref, logit_ref, stat_ref):
    words = own_ref.shape[0]
    total = jnp.zeros((1, 128), F32)
    for t in range(LIVE // 128):
        at = slice(t * 128, t * 128 + 128)
        logits = own_ref[:, at] + other_ref[:, at]
        logit_ref[:, at] = logits
        top = jnp.max(logits, axis=0, keepdims=True)
        stat_ref[t : t + 1, :] = top + jnp.log(jnp.sum(jnp.exp(logits - top), axis=0, keepdims=True))
        hit = lax.broadcasted_iota(jnp.int32, (words, 128), 0) == word_ref[:, at]
        chosen = jnp.sum(jnp.where(hit, logits, 0.0), axis=0, keepdims=True)
        spot = lax.broadcasted_iota(jnp.int32, (1, 128), 1) + t * 128
        total = total + jnp.where(spot.astype(F32) < count_ref[0], chosen, 0.0)
    stat_ref[5:8, :] = jnp.broadcast_to(jnp.sum(total, axis=1, keepdims=True), (3, 128))


def stats_of(count, own, other, word):
    words = own.shape[0]
    return pl.pallas_call(
        stats_kernel,
        name="stats",
        compiler_params=pltpu.CompilerParams(vmem_limit_bytes=6 * MIB),
        out_shape=(jax.ShapeDtypeStruct((words, LIVE), F32), jax.ShapeDtypeStruct((8, 128), F32)),
        in_specs=[SM] + [VM] * 3,
        out_specs=(VM, VM),
        cost_estimate=pl.CostEstimate(flops=8 * words * LIVE, bytes_accessed=12 * words * LIVE, transcendentals=words * LIVE),
    )(count, own, other, word)


def grad_kernel(logit_ref, total_ref, coef_ref, word_ref, out_ref):
    words = logit_ref.shape[0]
    for t in range(LIVE // 128):
        at = slice(t * 128, t * 128 + 128)
        hit = lax.broadcasted_iota(jnp.int32, (words, 128), 0) == word_ref[:, at]
        value = (jnp.exp(logit_ref[:, at] - total_ref[t : t + 1, :]) - hit.astype(F32)) * coef_ref[t : t + 1, :]
        out_ref[:, at] = value.astype(BF16)


def grad_of(logits, total, coef, word):
    words = logits.shape[0]
    return pl.pallas_call(
        grad_kernel,
        name="logit_grad",
        compiler_params=pltpu.CompilerParams(vmem_limit_bytes=4 * MIB),
        out_shape=jax.ShapeDtypeStruct((words, LIVE), BF16),
        in_specs=[VM] * 4,
        out_specs=VM,
        cost_estimate=pl.CostEstimate(flops=4 * words * LIVE, bytes_accessed=6 * words * LIVE, transcendentals=words * LIVE),
    )(logits, total, coef, word)


def finish_kernel(grad_ref, h_ref, gain_ref, out_ref, turned):
    slots, width = h_ref.shape
    for core in range(2):
        for part in range(2):
            for a in range(4):
                for b in range(2):
                    blocks = []
                    for pair in range(2):
                        for z in range(8):
                            other = 2 * b + pair
                            y, x = (other, a) if part == 0 else (a, other)
                            blocks.append(grad_ref[y, z, x, core, part])
                    at = core * (width // 2) + part * (width // 4) + a * 256 + b * 128
                    turned[:, at : at + 128] = jnp.concatenate(blocks, 0).T

    def step(i, carry):
        at = pl.ds(pl.multiple_of(i * 16, 16), 16)
        values = h_ref[at, :].astype(F32)
        scale = lax.rsqrt(jnp.sum(values * values, axis=1, keepdims=True) / width + EPSILON)
        pulled = turned[at, :] * gain_ref[...]
        inner = jnp.sum(values * pulled, axis=1, keepdims=True) / width
        out_ref[at, :] = (scale * pulled - scale * scale * scale * values * inner).astype(BF16)
        return carry

    lax.fori_loop(0, slots // 16, step, 0)


def finish(grad, rows, gain):
    slots, width = rows.shape
    vmem = pl.BlockSpec(memory_space=pltpu.VMEM)
    return pl.pallas_call(
        finish_kernel,
        out_shape=jax.ShapeDtypeStruct((slots, width), BF16),
        in_specs=[vmem] * 3,
        out_specs=vmem,
        scratch_shapes=[pltpu.VMEM((slots, width), F32)],
        compiler_params=pltpu.CompilerParams(vmem_limit_bytes=16 * MIB),
        cost_estimate=pl.CostEstimate(flops=8 * slots * width, bytes_accessed=8 * slots * width, transcendentals=slots),
    )(grad, rows, gain.reshape(1, width))


def merge_rows(rows):
    top = jnp.max(rows, axis=0)
    joined = top + jnp.log(jnp.sum(jnp.exp(rows - top[None]), axis=0))
    return jnp.where(jnp.arange(8)[:, None] < 5, joined, jnp.sum(rows, axis=0))


def body(hidden, norm_gain, out_weight, targets, loss_mask, slot_position, counts, loss_scale):
    slots, width = hidden.shape[1], hidden.shape[2]
    words = out_weight.shape[0]
    core, y = lax.axis_index("c"), lax.axis_index("y")
    offset = lax.axis_index(AXES) * words
    half = width // 2
    raw = hidden.reshape(slots, width)
    packed = slices_of(y.reshape(1).astype(jnp.int32), raw, norm_gain, targets, loss_mask, slot_position)
    packed, late_weight = lax.optimization_barrier((packed, out_weight))
    packed = exchange(packed, PIPE)
    mine = lax.dynamic_slice_in_dim(late_weight, core * half, half, 1)
    other = swap_cores(lax.dynamic_slice_in_dim(late_weight, (1 - core) * half, half, 1))

    near_one, near_two, word, column, coef, count = compact_of(
        offset.reshape(1).astype(jnp.int32), loss_scale.reshape(1), counts, packed
    )
    weight_total = count[0, 0]
    select = column.reshape(8 * slots, 1) == jnp.arange(LIVE, dtype=jnp.int32)[None, :]
    one = place(gather_ring(near_one, "x"), "x").reshape(1024, LIVE)
    two = place(gather_ring(near_two, "y"), "y").reshape(1024, LIVE)
    sib = product(other, one, two)
    sib, one, two = lax.optimization_barrier((sib, one, two))
    logits, stats = stats_of(weight_total.reshape(1), product(mine, one, two), swap_cores(sib), word)
    stats = merge_rows(everyone(stats, ("z", "y")))
    stats = merge_rows(everyone(stats, PIPE))
    weight = (jnp.arange(8 * slots, dtype=F32).reshape(8, slots) < weight_total).astype(F32)
    loss = (jnp.sum((weight * stats)[:5]) - stats[5, 0]) / weight_total
    logit_grad = grad_of(logits, stats, coef, word)
    other_grad = swap_cores(logit_grad)
    grad = pull(mine, other, logit_grad, other_grad)

    one = scatter_ring(grad[:1024].reshape(4, 256, LIVE), "x")
    two = scatter_ring(grad[1024:].reshape(4, 256, LIVE), "y")
    one = scatter_direct(one.reshape(4, 64, LIVE), "y")
    two = scatter_direct(two.reshape(4, 64, LIVE), "x")
    chunk = jnp.concatenate([one.reshape(8, 8, LIVE), two.reshape(8, 8, LIVE)], 1).reshape(128, LIVE)
    spread = lax.dot_general(
        chunk, select.astype(F32), NT, precision=lax.Precision.HIGHEST, preferred_element_type=F32
    )
    spread = spread.astype(F16).reshape(8, 16, 8, slots).transpose(2, 0, 1, 3).reshape(64, 16, slots)
    spread = exchange(spread, ("x", "c", "z")).reshape(8, 8, 16, slots)
    spread = jnp.sum(spread.astype(F32), axis=1).astype(F16).reshape(128, slots)
    full = everyone(spread, ("z",)).reshape(1024, slots)
    full = place(gather_ring(full, "y"), "y").astype(F32).reshape(4, 8, 4, 2, 2, 8, slots)
    return loss, finish(full, raw, norm_gain).reshape(1, slots, width)


def solution(mesh):
    split = Mesh(mesh.devices.reshape(4, 2, 8, 4), AXES)
    return jax.shard_map(
        body,
        mesh=split,
        in_specs=(
            P(PIPE, None, None),
            P(),
            P(AXES, None),
            P(PIPE, None),
            P(PIPE, None),
            P(PIPE, None),
            P(),
            P(),
        ),
        out_specs=(P(), P(PIPE, None, None)),
        check_vma=False,
    )
```

```python
import jax
import jax.numpy as jnp
from jax import lax
from jax.experimental import pallas as pl
from jax.experimental.pallas import tpu as pltpu
from jax.sharding import Mesh
from jax.sharding import PartitionSpec as P

AXES = ("x", "c", "z", "y")
SIZE = {"x": 4, "c": 2, "z": 8, "y": 4}
PIPE = ("x", "c")
LIVE = 640
EPSILON = 1e-05
BF16, F16, F32 = jnp.bfloat16, jnp.float16, jnp.float32


def shift(value, axis, by):
    n = SIZE[axis]
    return lax.ppermute(value, axis, [(i, (i + by) % n) for i in range(n)])


def swap_cores(value):
    return lax.ppermute(value, "c", [(0, 1), (1, 0)])


def place(pieces, axis):
    own = lax.axis_index(axis)
    out = jnp.zeros((4,) + pieces[0].shape, pieces[0].dtype)
    for k, piece in enumerate(pieces):
        out = lax.dynamic_update_index_in_dim(out, piece, (own + k) % 4, 0)
    return out


def gather_ring(chunk, axis):
    half = chunk.shape[0] // 2
    below, above = shift(chunk, axis, 1), shift(chunk, axis, -1)
    first, second = shift(below[:half], axis, 1), shift(above[half:], axis, -1)
    return [chunk, above, jnp.concatenate([first, second], 0), below]


def pick(chunks, axis, k):
    own = lax.axis_index(axis)
    return lax.dynamic_index_in_dim(chunks, (own + k) % 4, 0, keepdims=False)


def scatter_direct(chunks, axis):
    got = [shift(pick(chunks, axis, k).astype(F16), axis, k) for k in (1, 2, 3)]
    total = pick(chunks, axis, 0)
    for g in got:
        total = total + g.astype(F32)
    return total


def scatter_ring(chunks, axis):
    half = chunks.shape[1] // 2
    far = pick(chunks, axis, 2).astype(F16)
    first, second = shift(far[:half], axis, 1), shift(far[half:], axis, -1)
    up, down = pick(chunks, axis, 1), pick(chunks, axis, 3)
    up = jnp.concatenate([up[:half] + first.astype(F32), up[half:]], 0).astype(F16)
    down = jnp.concatenate([down[:half], down[half:] + second.astype(F32)], 0).astype(F16)
    got_below, got_above = shift(up, axis, 1), shift(down, axis, -1)
    return pick(chunks, axis, 0) + got_below.astype(F32) + got_above.astype(F32)


def exchange(value, axes):
    return lax.all_to_all(value, axes, 0, 0)


def everyone(value, axes):
    n = 1
    for a in axes:
        n *= SIZE[a]
    return exchange(jnp.broadcast_to(value[None], (n,) + value.shape), axes)


def merge(stats):
    top = jnp.max(stats[:, 0], axis=0)
    total = jnp.sum(stats[:, 1] * jnp.exp(stats[:, 0] - top[None]), axis=0)
    return jnp.stack([top, total, jnp.sum(stats[:, 2], axis=0)])


NT = (((1,), (1,)), ((), ()))
TN = (((0,), (0,)), ((), ()))
MIB = 1024 * 1024
VM, SM = pl.BlockSpec(memory_space=pltpu.VMEM), pl.BlockSpec(memory_space=pltpu.SMEM)


def slice_kernel(y_ref, h_ref, gain_ref, target_ref, mask_ref, position_ref, out_ref, scales):
    slots, width = h_ref.shape
    half, quarter = width // 2, width // 4

    def step(i, carry):
        at = pl.ds(pl.multiple_of(i * 16, 16), 16)
        values = h_ref[at, :].astype(F32)
        mean = jnp.sum(values * values, axis=1, keepdims=True) / width
        scales[at, :] = jnp.broadcast_to(lax.rsqrt(mean + EPSILON), (16, 128))
        return carry

    lax.fori_loop(0, slots // 16, step, 0)

    def tile(offset):
        at = pl.ds(pl.multiple_of(offset, 128), 128)
        return (h_ref[:, at].astype(F32) * scales[...] * gain_ref[:, at]).astype(BF16).T

    word = target_ref[...]
    rows = [word & 255, (word >> 8) & 255, word >> 16, mask_ref[...], position_ref[...]]
    info = jnp.concatenate(rows + [jnp.zeros_like(word)] * 11, 0).astype(F32).astype(BF16)

    def fill(core, carry):
        for part in range(2):
            for x in range(4):
                out_ref[x * 2 + core, part * 128 : part * 128 + 128, :] = tile(core * half + x * 256 + part * 128)
                out_ref[x * 2 + core, 512:528, :] = info
            second = tile(core * half + quarter + y_ref[0] * 256 + part * 128)
            for x in range(4):
                out_ref[x * 2 + core, 256 + part * 128 : 384 + part * 128, :] = second
        return carry

    lax.fori_loop(0, 2, fill, 0)


def slices_of(y, rows, gain, targets, mask, position):
    slots, width = rows.shape
    return pl.pallas_call(
        slice_kernel,
        name="normed_slices",
        out_shape=jax.ShapeDtypeStruct((8, 528, slots), BF16),
        in_specs=[SM] + [VM] * 5,
        out_specs=VM,
        scratch_shapes=[pltpu.VMEM((slots, 128), F32)],
        cost_estimate=pl.CostEstimate(flops=4 * slots * width, bytes_accessed=4 * slots * width, transcendentals=slots),
    )(y, rows, gain.reshape(1, width), targets, mask, position)


def compact_kernel(offset_ref, loss_scale_ref, counts_ref, packed_ref, one_ref, two_ref, word_ref, column_ref, coef_ref, count_ref, acc):
    iota = lambda shape, axis: lax.broadcasted_iota(jnp.int32, shape, axis)
    rows = []
    for micro in range(8):
        codes = packed_ref[micro, 512:528, :].astype(F32)
        rows.append(((codes[4:5] < counts_ref[micro].astype(F32)) & (codes[3:4] == 1.0)).astype(F32))
    live = jnp.concatenate(rows, 0)
    before = jnp.dot(
        live.astype(BF16),
        jnp.where(iota((128, 128), 0) < iota((128, 128), 1), 1.0, 0.0).astype(BF16),
        preferred_element_type=F32,
    )
    per_micro = jnp.sum(live, axis=1, keepdims=True)
    base = [jnp.zeros((1, 1), F32)]
    for micro in range(8):
        base.append(base[-1] + per_micro[micro : micro + 1])
    count = base.pop()
    column = jnp.where(live > 0.0, before + jnp.concatenate(base, 0), -1.0).astype(jnp.int32)
    column_ref[...] = column
    spot = iota((8, 128), 0) * 128 + iota((8, 128), 1)
    coef_ref[...] = jnp.where(spot.astype(F32) < count, loss_scale_ref[0] / count, 0.0)
    count_ref[...] = jnp.broadcast_to(count, (8, 128))
    for n in range(4):
        values = jnp.concatenate([packed_ref[2 * n], packed_ref[2 * n + 1]], 1)
        places = [
            jnp.where(iota((LIVE, 128), 0) == column[m : m + 1], 1.0, 0.0).astype(BF16) for m in (2 * n, 2 * n + 1)
        ]
        part = lax.dot_general(values, jnp.concatenate(places, 1), NT, preferred_element_type=F32)
        acc[...] = part if n == 0 else acc[...] + part
    one_ref[...] = acc[0:256, :].astype(BF16)
    two_ref[...] = acc[256:512, :].astype(BF16)
    word = acc[512:513, :] + 256.0 * acc[513:514, :] + 65536.0 * acc[514:515, :]
    word_ref[...] = word.astype(jnp.int32) - offset_ref[0]


def compact_of(offset, loss_scale, counts, packed):
    tile, whole = jax.ShapeDtypeStruct((8, 128), F32), jax.ShapeDtypeStruct((8, 128), jnp.int32)
    wide = jax.ShapeDtypeStruct((256, LIVE), BF16)
    return pl.pallas_call(
        compact_kernel,
        name="compact",
        out_shape=(wide, wide, jax.ShapeDtypeStruct((1, LIVE), jnp.int32), whole, tile, tile),
        in_specs=[SM, SM, SM, VM],
        out_specs=(VM,) * 6,
        scratch_shapes=[pltpu.VMEM((528, LIVE), F32)],
        compiler_params=pltpu.CompilerParams(vmem_limit_bytes=12 * MIB),
        cost_estimate=pl.CostEstimate(flops=2 * 528 * 1024 * LIVE, bytes_accessed=3 * MIB, transcendentals=0),
    )(offset, loss_scale, counts, packed)


def product_kernel(weight_ref, one_ref, two_ref, out_ref):
    width = one_ref.shape[0]
    for at in (slice(0, 256), slice(256, 512), slice(512, 640)):
        out_ref[:, at] = jnp.dot(weight_ref[:, :width], one_ref[:, at], preferred_element_type=F32) + jnp.dot(
            weight_ref[:, width:], two_ref[:, at], preferred_element_type=F32
        )


def product(weight, one, two):
    words, width = weight.shape
    return pl.pallas_call(
        product_kernel,
        name="product",
        out_shape=jax.ShapeDtypeStruct((words, LIVE), F32),
        in_specs=[VM] * 3,
        out_specs=VM,
        compiler_params=pltpu.CompilerParams(vmem_limit_bytes=10 * MIB),
        cost_estimate=pl.CostEstimate(flops=2 * words * width * LIVE, bytes_accessed=6 * MIB, transcendentals=0),
    )(weight, one, two)


def pull_kernel(mine_ref, other_ref, grad_ref, other_grad_ref, out_ref):
    def step(i, carry):
        at = pl.ds(pl.multiple_of(i * 512, 512), 512)
        out_ref[at, :] = lax.dot_general(
            mine_ref[:, at], grad_ref[...], TN, preferred_element_type=F32
        ) + lax.dot_general(other_ref[:, at], other_grad_ref[...], TN, preferred_element_type=F32)
        return carry

    lax.fori_loop(0, out_ref.shape[0] // 512, step, 0)


def pull(mine, other, grad, other_grad):
    words, width = mine.shape
    return pl.pallas_call(
        pull_kernel,
        name="pull",
        out_shape=jax.ShapeDtypeStruct((width, LIVE), F32),
        in_specs=[VM] * 4,
        out_specs=VM,
        compiler_params=pltpu.CompilerParams(vmem_limit_bytes=14 * MIB),
        cost_estimate=pl.CostEstimate(flops=4 * words * width * LIVE, bytes_accessed=12 * MIB, transcendentals=0),
    )(mine, other, grad, other_grad)


def stats_kernel(count_ref, own_ref, other_ref, word_ref, logit_ref, stat_ref):
    words = own_ref.shape[0]
    total = jnp.zeros((1, 128), F32)
    for t in range(LIVE // 128):
        at = slice(t * 128, t * 128 + 128)
        logits = own_ref[:, at] + other_ref[:, at]
        logit_ref[:, at] = logits
        top = jnp.max(logits, axis=0, keepdims=True)
        stat_ref[t : t + 1, :] = top + jnp.log(jnp.sum(jnp.exp(logits - top), axis=0, keepdims=True))
        hit = lax.broadcasted_iota(jnp.int32, (words, 128), 0) == word_ref[:, at]
        chosen = jnp.sum(jnp.where(hit, logits, 0.0), axis=0, keepdims=True)
        spot = lax.broadcasted_iota(jnp.int32, (1, 128), 1) + t * 128
        total = total + jnp.where(spot.astype(F32) < count_ref[0], chosen, 0.0)
    stat_ref[5:8, :] = jnp.broadcast_to(jnp.sum(total, axis=1, keepdims=True), (3, 128))


def stats_of(count, own, other, word):
    words = own.shape[0]
    return pl.pallas_call(
        stats_kernel,
        name="stats",
        compiler_params=pltpu.CompilerParams(vmem_limit_bytes=6 * MIB),
        out_shape=(jax.ShapeDtypeStruct((words, LIVE), F32), jax.ShapeDtypeStruct((8, 128), F32)),
        in_specs=[SM] + [VM] * 3,
        out_specs=(VM, VM),
        cost_estimate=pl.CostEstimate(flops=8 * words * LIVE, bytes_accessed=12 * words * LIVE, transcendentals=words * LIVE),
    )(count, own, other, word)


def grad_kernel(logit_ref, total_ref, coef_ref, word_ref, out_ref):
    words = logit_ref.shape[0]
    for t in range(LIVE // 128):
        at = slice(t * 128, t * 128 + 128)
        hit = lax.broadcasted_iota(jnp.int32, (words, 128), 0) == word_ref[:, at]
        value = (jnp.exp(logit_ref[:, at] - total_ref[t : t + 1, :]) - hit.astype(F32)) * coef_ref[t : t + 1, :]
        out_ref[:, at] = value.astype(BF16)


def grad_of(logits, total, coef, word):
    words = logits.shape[0]
    return pl.pallas_call(
        grad_kernel,
        name="logit_grad",
        compiler_params=pltpu.CompilerParams(vmem_limit_bytes=4 * MIB),
        out_shape=jax.ShapeDtypeStruct((words, LIVE), BF16),
        in_specs=[VM] * 4,
        out_specs=VM,
        cost_estimate=pl.CostEstimate(flops=4 * words * LIVE, bytes_accessed=6 * words * LIVE, transcendentals=words * LIVE),
    )(logits, total, coef, word)


def finish_kernel(grad_ref, h_ref, gain_ref, out_ref, turned):
    slots, width = h_ref.shape
    for core in range(2):
        for part in range(2):
            for a in range(4):
                for b in range(2):
                    blocks = []
                    for pair in range(2):
                        for z in range(8):
                            other = 2 * b + pair
                            y, x = (other, a) if part == 0 else (a, other)
                            blocks.append(grad_ref[y, z, x, core, part])
                    at = core * (width // 2) + part * (width // 4) + a * 256 + b * 128
                    turned[:, at : at + 128] = jnp.concatenate(blocks, 0).T

    def step(i, carry):
        at = pl.ds(pl.multiple_of(i * 16, 16), 16)
        values = h_ref[at, :].astype(F32)
        scale = lax.rsqrt(jnp.sum(values * values, axis=1, keepdims=True) / width + EPSILON)
        pulled = turned[at, :] * gain_ref[...]
        inner = jnp.sum(values * pulled, axis=1, keepdims=True) / width
        out_ref[at, :] = (scale * pulled - scale * scale * scale * values * inner).astype(BF16)
        return carry

    lax.fori_loop(0, slots // 16, step, 0)


def finish(grad, rows, gain):
    slots, width = rows.shape
    vmem = pl.BlockSpec(memory_space=pltpu.VMEM)
    return pl.pallas_call(
        finish_kernel,
        out_shape=jax.ShapeDtypeStruct((slots, width), BF16),
        in_specs=[vmem] * 3,
        out_specs=vmem,
        scratch_shapes=[pltpu.VMEM((slots, width), F32)],
        compiler_params=pltpu.CompilerParams(vmem_limit_bytes=16 * MIB),
        cost_estimate=pl.CostEstimate(flops=8 * slots * width, bytes_accessed=8 * slots * width, transcendentals=slots),
    )(grad, rows, gain.reshape(1, width))


def merge_rows(rows):
    top = jnp.max(rows, axis=0)
    joined = top + jnp.log(jnp.sum(jnp.exp(rows - top[None]), axis=0))
    return jnp.where(jnp.arange(8)[:, None] < 5, joined, jnp.sum(rows, axis=0))


def body(hidden, norm_gain, out_weight, targets, loss_mask, slot_position, counts, loss_scale):
    slots, width = hidden.shape[1], hidden.shape[2]
    words = out_weight.shape[0]
    core, y = lax.axis_index("c"), lax.axis_index("y")
    offset = lax.axis_index(AXES) * words
    half = width // 2
    raw = hidden.reshape(slots, width)
    packed = slices_of(y.reshape(1).astype(jnp.int32), raw, norm_gain, targets, loss_mask, slot_position)
    packed, late_weight = lax.optimization_barrier((packed, out_weight))
    packed = exchange(packed, PIPE)
    mine = lax.dynamic_slice_in_dim(late_weight, core * half, half, 1)
    other = swap_cores(lax.dynamic_slice_in_dim(late_weight, (1 - core) * half, half, 1))

    near_one, near_two, word, column, coef, count = compact_of(
        offset.reshape(1).astype(jnp.int32), loss_scale.reshape(1), counts, packed
    )
    weight_total = count[0, 0]
    select = column.reshape(8 * slots, 1) == jnp.arange(LIVE, dtype=jnp.int32)[None, :]
    one = place(gather_ring(near_one, "x"), "x").reshape(1024, LIVE)
    two = place(gather_ring(near_two, "y"), "y").reshape(1024, LIVE)
    sib = product(other, one, two)
    sib, one, two = lax.optimization_barrier((sib, one, two))
    logits, stats = stats_of(weight_total.reshape(1), product(mine, one, two), swap_cores(sib), word)
    stats = merge_rows(everyone(stats, ("z",)))
    stats = merge_rows(everyone(stats, ("x", "c", "y")))
    weight = (jnp.arange(8 * slots, dtype=F32).reshape(8, slots) < weight_total).astype(F32)
    loss = (jnp.sum((weight * stats)[:5]) - stats[5, 0]) / weight_total
    logit_grad = grad_of(logits, stats, coef, word)
    other_grad = swap_cores(logit_grad)
    grad = pull(mine, other, logit_grad, other_grad)

    one = scatter_ring(grad[:1024].reshape(4, 256, LIVE), "x")
    two = scatter_ring(grad[1024:].reshape(4, 256, LIVE), "y")
    one = scatter_direct(one.reshape(4, 64, LIVE), "y")
    two = scatter_direct(two.reshape(4, 64, LIVE), "x")
    chunk = jnp.concatenate([one.reshape(8, 8, LIVE), two.reshape(8, 8, LIVE)], 1).reshape(128, LIVE)
    spread = lax.dot_general(
        chunk, select.astype(F32), NT, precision=lax.Precision.HIGHEST, preferred_element_type=F32
    )
    spread = spread.astype(F16).reshape(8, 16, 8, slots).transpose(2, 0, 1, 3).reshape(64, 16, slots)
    spread = exchange(spread, ("x", "c", "z")).reshape(8, 8, 16, slots)
    spread = jnp.sum(spread.astype(F32), axis=1).astype(F16).reshape(128, slots)
    full = everyone(spread, ("z",)).reshape(1024, slots)
    full = place(gather_ring(full, "y"), "y").astype(F32).reshape(4, 8, 4, 2, 2, 8, slots)
    return loss, finish(full, raw, norm_gain).reshape(1, slots, width)


def solution(mesh):
    split = Mesh(mesh.devices.reshape(4, 2, 8, 4), AXES)
    return jax.shard_map(
        body,
        mesh=split,
        in_specs=(
            P(PIPE, None, None),
            P(),
            P(AXES, None),
            P(PIPE, None),
            P(PIPE, None),
            P(PIPE, None),
            P(),
            P(),
        ),
        out_specs=(P(), P(PIPE, None, None)),
        check_vma=False,
    )
```

```python
import jax
import jax.numpy as jnp
from jax import lax
from jax.experimental import pallas as pl
from jax.experimental.pallas import tpu as pltpu
from jax.sharding import Mesh
from jax.sharding import PartitionSpec as P

AXES = ("x", "c", "z", "y")
SIZE = {"x": 4, "c": 2, "z": 8, "y": 4}
PIPE = ("x", "c")
LIVE = 640
EPSILON = 1e-05
BF16, F16, F32 = jnp.bfloat16, jnp.float16, jnp.float32


def shift(value, axis, by):
    n = SIZE[axis]
    return lax.ppermute(value, axis, [(i, (i + by) % n) for i in range(n)])


def swap_cores(value):
    return lax.ppermute(value, "c", [(0, 1), (1, 0)])


def place(pieces, axis):
    own = lax.axis_index(axis)
    out = jnp.zeros((4,) + pieces[0].shape, pieces[0].dtype)
    for k, piece in enumerate(pieces):
        out = lax.dynamic_update_index_in_dim(out, piece, (own + k) % 4, 0)
    return out


def gather_ring(chunk, axis):
    half = chunk.shape[0] // 2
    below, above = shift(chunk, axis, 1), shift(chunk, axis, -1)
    first, second = shift(below[:half], axis, 1), shift(above[half:], axis, -1)
    return [chunk, above, jnp.concatenate([first, second], 0), below]


def pick(chunks, axis, k):
    own = lax.axis_index(axis)
    return lax.dynamic_index_in_dim(chunks, (own + k) % 4, 0, keepdims=False)


def scatter_direct(chunks, axis):
    got = [shift(pick(chunks, axis, k).astype(F16), axis, k) for k in (1, 2, 3)]
    total = pick(chunks, axis, 0)
    for g in got:
        total = total + g.astype(F32)
    return total


def scatter_ring(chunks, axis):
    half = chunks.shape[1] // 2
    far = pick(chunks, axis, 2).astype(F16)
    first, second = shift(far[:half], axis, 1), shift(far[half:], axis, -1)
    up, down = pick(chunks, axis, 1), pick(chunks, axis, 3)
    up = jnp.concatenate([up[:half] + first.astype(F32), up[half:]], 0).astype(F16)
    down = jnp.concatenate([down[:half], down[half:] + second.astype(F32)], 0).astype(F16)
    got_below, got_above = shift(up, axis, 1), shift(down, axis, -1)
    return pick(chunks, axis, 0) + got_below.astype(F32) + got_above.astype(F32)


def exchange(value, axes):
    return lax.all_to_all(value, axes, 0, 0)


def everyone(value, axes):
    n = 1
    for a in axes:
        n *= SIZE[a]
    return exchange(jnp.broadcast_to(value[None], (n,) + value.shape), axes)


def merge(stats):
    top = jnp.max(stats[:, 0], axis=0)
    total = jnp.sum(stats[:, 1] * jnp.exp(stats[:, 0] - top[None]), axis=0)
    return jnp.stack([top, total, jnp.sum(stats[:, 2], axis=0)])


NT = (((1,), (1,)), ((), ()))
TN = (((0,), (0,)), ((), ()))
MIB = 1024 * 1024
VM, SM = pl.BlockSpec(memory_space=pltpu.VMEM), pl.BlockSpec(memory_space=pltpu.SMEM)


def slice_kernel(y_ref, h_ref, gain_ref, target_ref, mask_ref, position_ref, out_ref, scales):
    slots, width = h_ref.shape
    half, quarter = width // 2, width // 4

    def step(i, carry):
        at = pl.ds(pl.multiple_of(i * 16, 16), 16)
        values = h_ref[at, :].astype(F32)
        mean = jnp.sum(values * values, axis=1, keepdims=True) / width
        scales[at, :] = jnp.broadcast_to(lax.rsqrt(mean + EPSILON), (16, 128))
        return carry

    lax.fori_loop(0, slots // 16, step, 0)

    def tile(offset):
        at = pl.ds(pl.multiple_of(offset, 128), 128)
        return (h_ref[:, at].astype(F32) * scales[...] * gain_ref[:, at]).astype(BF16).T

    word = target_ref[...]
    rows = [word & 255, (word >> 8) & 255, word >> 16, mask_ref[...], position_ref[...]]
    info = jnp.concatenate(rows + [jnp.zeros_like(word)] * 11, 0).astype(F32).astype(BF16)

    def fill(core, carry):
        for part in range(2):
            for x in range(4):
                out_ref[x * 2 + core, part * 128 : part * 128 + 128, :] = tile(core * half + x * 256 + part * 128)
                out_ref[x * 2 + core, 512:528, :] = info
            second = tile(core * half + quarter + y_ref[0] * 256 + part * 128)
            for x in range(4):
                out_ref[x * 2 + core, 256 + part * 128 : 384 + part * 128, :] = second
        return carry

    lax.fori_loop(0, 2, fill, 0)


def slices_of(y, rows, gain, targets, mask, position):
    slots, width = rows.shape
    return pl.pallas_call(
        slice_kernel,
        name="normed_slices",
        out_shape=jax.ShapeDtypeStruct((8, 528, slots), BF16),
        in_specs=[SM] + [VM] * 5,
        out_specs=VM,
        scratch_shapes=[pltpu.VMEM((slots, 128), F32)],
        cost_estimate=pl.CostEstimate(flops=4 * slots * width, bytes_accessed=4 * slots * width, transcendentals=slots),
    )(y, rows, gain.reshape(1, width), targets, mask, position)


def compact_kernel(offset_ref, loss_scale_ref, counts_ref, packed_ref, one_ref, two_ref, word_ref, column_ref, coef_ref, count_ref, acc):
    iota = lambda shape, axis: lax.broadcasted_iota(jnp.int32, shape, axis)
    rows = []
    for micro in range(8):
        codes = packed_ref[micro, 512:528, :].astype(F32)
        rows.append(((codes[4:5] < counts_ref[micro].astype(F32)) & (codes[3:4] == 1.0)).astype(F32))
    live = jnp.concatenate(rows, 0)
    before = jnp.dot(
        live.astype(BF16),
        jnp.where(iota((128, 128), 0) < iota((128, 128), 1), 1.0, 0.0).astype(BF16),
        preferred_element_type=F32,
    )
    per_micro = jnp.sum(live, axis=1, keepdims=True)
    base = [jnp.zeros((1, 1), F32)]
    for micro in range(8):
        base.append(base[-1] + per_micro[micro : micro + 1])
    count = base.pop()
    column = jnp.where(live > 0.0, before + jnp.concatenate(base, 0), -1.0).astype(jnp.int32)
    column_ref[...] = column
    spot = iota((8, 128), 0) * 128 + iota((8, 128), 1)
    coef_ref[...] = jnp.where(spot.astype(F32) < count, loss_scale_ref[0] / count, 0.0)
    count_ref[...] = jnp.broadcast_to(count, (8, 128))
    acc[...] = jnp.zeros_like(acc)

    def add(n, carry):
        values = jnp.concatenate([packed_ref[2 * n], packed_ref[2 * n + 1]], 1)
        places = [
            jnp.where(iota((LIVE, 128), 0) == column_ref[pl.ds(2 * n + k, 1), :], 1.0, 0.0).astype(BF16) for k in range(2)
        ]
        acc[...] += lax.dot_general(values, jnp.concatenate(places, 1), NT, preferred_element_type=F32)
        return carry

    lax.fori_loop(0, 4, add, 0)
    one_ref[...] = acc[0:256, :].astype(BF16)
    two_ref[...] = acc[256:512, :].astype(BF16)
    word = acc[512:513, :] + 256.0 * acc[513:514, :] + 65536.0 * acc[514:515, :]
    word_ref[...] = word.astype(jnp.int32) - offset_ref[0]


def compact_of(offset, loss_scale, counts, packed):
    tile, whole = jax.ShapeDtypeStruct((8, 128), F32), jax.ShapeDtypeStruct((8, 128), jnp.int32)
    wide = jax.ShapeDtypeStruct((256, LIVE), BF16)
    return pl.pallas_call(
        compact_kernel,
        name="compact",
        out_shape=(wide, wide, jax.ShapeDtypeStruct((1, LIVE), jnp.int32), whole, tile, tile),
        in_specs=[SM, SM, SM, VM],
        out_specs=(VM,) * 6,
        scratch_shapes=[pltpu.VMEM((528, LIVE), F32)],
        compiler_params=pltpu.CompilerParams(vmem_limit_bytes=12 * MIB),
        cost_estimate=pl.CostEstimate(flops=2 * 528 * 1024 * LIVE, bytes_accessed=3 * MIB, transcendentals=0),
    )(offset, loss_scale, counts, packed)


def product_kernel(weight_ref, one_ref, two_ref, out_ref):
    width = one_ref.shape[0]
    for at in (slice(0, 256), slice(256, 512), slice(512, 640)):
        out_ref[:, at] = jnp.dot(weight_ref[:, :width], one_ref[:, at], preferred_element_type=F32) + jnp.dot(
            weight_ref[:, width:], two_ref[:, at], preferred_element_type=F32
        )


def product(weight, one, two):
    words, width = weight.shape
    return pl.pallas_call(
        product_kernel,
        name="product",
        out_shape=jax.ShapeDtypeStruct((words, LIVE), F32),
        in_specs=[VM] * 3,
        out_specs=VM,
        compiler_params=pltpu.CompilerParams(vmem_limit_bytes=10 * MIB),
        cost_estimate=pl.CostEstimate(flops=2 * words * width * LIVE, bytes_accessed=6 * MIB, transcendentals=0),
    )(weight, one, two)


def pull_kernel(mine_ref, other_ref, grad_ref, other_grad_ref, out_ref):
    def step(i, carry):
        at = pl.ds(pl.multiple_of(i * 512, 512), 512)
        out_ref[at, :] = lax.dot_general(
            mine_ref[:, at], grad_ref[...], TN, preferred_element_type=F32
        ) + lax.dot_general(other_ref[:, at], other_grad_ref[...], TN, preferred_element_type=F32)
        return carry

    lax.fori_loop(0, out_ref.shape[0] // 512, step, 0)


def pull(mine, other, grad, other_grad):
    words, width = mine.shape
    return pl.pallas_call(
        pull_kernel,
        name="pull",
        out_shape=jax.ShapeDtypeStruct((width, LIVE), F32),
        in_specs=[VM] * 4,
        out_specs=VM,
        compiler_params=pltpu.CompilerParams(vmem_limit_bytes=14 * MIB),
        cost_estimate=pl.CostEstimate(flops=4 * words * width * LIVE, bytes_accessed=12 * MIB, transcendentals=0),
    )(mine, other, grad, other_grad)


def stats_kernel(count_ref, own_ref, other_ref, word_ref, logit_ref, stat_ref):
    words = own_ref.shape[0]
    total = jnp.zeros((1, 128), F32)
    for t in range(LIVE // 128):
        at = slice(t * 128, t * 128 + 128)
        logits = own_ref[:, at] + other_ref[:, at]
        logit_ref[:, at] = logits
        top = jnp.max(logits, axis=0, keepdims=True)
        stat_ref[t : t + 1, :] = top + jnp.log(jnp.sum(jnp.exp(logits - top), axis=0, keepdims=True))
        hit = lax.broadcasted_iota(jnp.int32, (words, 128), 0) == word_ref[:, at]
        chosen = jnp.sum(jnp.where(hit, logits, 0.0), axis=0, keepdims=True)
        spot = lax.broadcasted_iota(jnp.int32, (1, 128), 1) + t * 128
        total = total + jnp.where(spot.astype(F32) < count_ref[0], chosen, 0.0)
    stat_ref[5:8, :] = jnp.broadcast_to(jnp.sum(total, axis=1, keepdims=True), (3, 128))


def stats_of(count, own, other, word):
    words = own.shape[0]
    return pl.pallas_call(
        stats_kernel,
        name="stats",
        compiler_params=pltpu.CompilerParams(vmem_limit_bytes=6 * MIB),
        out_shape=(jax.ShapeDtypeStruct((words, LIVE), F32), jax.ShapeDtypeStruct((8, 128), F32)),
        in_specs=[SM] + [VM] * 3,
        out_specs=(VM, VM),
        cost_estimate=pl.CostEstimate(flops=8 * words * LIVE, bytes_accessed=12 * words * LIVE, transcendentals=words * LIVE),
    )(count, own, other, word)


def grad_kernel(logit_ref, total_ref, coef_ref, word_ref, out_ref):
    words = logit_ref.shape[0]
    for t in range(LIVE // 128):
        at = slice(t * 128, t * 128 + 128)
        hit = lax.broadcasted_iota(jnp.int32, (words, 128), 0) == word_ref[:, at]
        value = (jnp.exp(logit_ref[:, at] - total_ref[t : t + 1, :]) - hit.astype(F32)) * coef_ref[t : t + 1, :]
        out_ref[:, at] = value.astype(BF16)


def grad_of(logits, total, coef, word):
    words = logits.shape[0]
    return pl.pallas_call(
        grad_kernel,
        name="logit_grad",
        compiler_params=pltpu.CompilerParams(vmem_limit_bytes=4 * MIB),
        out_shape=jax.ShapeDtypeStruct((words, LIVE), BF16),
        in_specs=[VM] * 4,
        out_specs=VM,
        cost_estimate=pl.CostEstimate(flops=4 * words * LIVE, bytes_accessed=6 * words * LIVE, transcendentals=words * LIVE),
    )(logits, total, coef, word)


def finish_kernel(grad_ref, h_ref, gain_ref, out_ref, turned):
    slots, width = h_ref.shape
    def turn(a, carry):
        for core in range(2):
            for part in range(2):
                for b in range(2):
                    blocks = []
                    for pair in range(2):
                        for z in range(8):
                            other = 2 * b + pair
                            y, x = (other, a) if part == 0 else (a, other)
                            blocks.append(grad_ref[y, z, x, core, part])
                    at = core * (width // 2) + part * (width // 4) + a * 256 + b * 128
                    turned[:, pl.ds(pl.multiple_of(at, 128), 128)] = jnp.concatenate(blocks, 0).T
        return carry

    lax.fori_loop(0, 4, turn, 0)

    def step(i, carry):
        at = pl.ds(pl.multiple_of(i * 16, 16), 16)
        values = h_ref[at, :].astype(F32)
        scale = lax.rsqrt(jnp.sum(values * values, axis=1, keepdims=True) / width + EPSILON)
        pulled = turned[at, :] * gain_ref[...]
        inner = jnp.sum(values * pulled, axis=1, keepdims=True) / width
        out_ref[at, :] = (scale * pulled - scale * scale * scale * values * inner).astype(BF16)
        return carry

    lax.fori_loop(0, slots // 16, step, 0)


def finish(grad, rows, gain):
    slots, width = rows.shape
    vmem = pl.BlockSpec(memory_space=pltpu.VMEM)
    return pl.pallas_call(
        finish_kernel,
        out_shape=jax.ShapeDtypeStruct((slots, width), BF16),
        in_specs=[vmem] * 3,
        out_specs=vmem,
        scratch_shapes=[pltpu.VMEM((slots, width), F32)],
        compiler_params=pltpu.CompilerParams(vmem_limit_bytes=16 * MIB),
        cost_estimate=pl.CostEstimate(flops=8 * slots * width, bytes_accessed=8 * slots * width, transcendentals=slots),
    )(grad, rows, gain.reshape(1, width))


def merge_rows(rows):
    top = jnp.max(rows, axis=0)
    joined = top + jnp.log(jnp.sum(jnp.exp(rows - top[None]), axis=0))
    return jnp.where(jnp.arange(8)[:, None] < 5, joined, jnp.sum(rows, axis=0))


def body(hidden, norm_gain, out_weight, targets, loss_mask, slot_position, counts, loss_scale):
    slots, width = hidden.shape[1], hidden.shape[2]
    words = out_weight.shape[0]
    core, y = lax.axis_index("c"), lax.axis_index("y")
    offset = lax.axis_index(AXES) * words
    half = width // 2
    raw = hidden.reshape(slots, width)
    packed = slices_of(y.reshape(1).astype(jnp.int32), raw, norm_gain, targets, loss_mask, slot_position)
    packed, late_weight = lax.optimization_barrier((packed, out_weight))
    packed = exchange(packed, PIPE)
    mine = lax.dynamic_slice_in_dim(late_weight, core * half, half, 1)
    other = swap_cores(lax.dynamic_slice_in_dim(late_weight, (1 - core) * half, half, 1))

    near_one, near_two, word, column, coef, count = compact_of(
        offset.reshape(1).astype(jnp.int32), loss_scale.reshape(1), counts, packed
    )
    weight_total = count[0, 0]
    select = column.reshape(8 * slots, 1) == jnp.arange(LIVE, dtype=jnp.int32)[None, :]
    one = place(gather_ring(near_one, "x"), "x").reshape(1024, LIVE)
    two = place(gather_ring(near_two, "y"), "y").reshape(1024, LIVE)
    sib = product(other, one, two)
    sib, one, two = lax.optimization_barrier((sib, one, two))
    logits, stats = stats_of(weight_total.reshape(1), product(mine, one, two), swap_cores(sib), word)
    stats = merge_rows(everyone(stats, ("z",)))
    stats = merge_rows(everyone(stats, ("x", "c", "y")))
    weight = (jnp.arange(8 * slots, dtype=F32).reshape(8, slots) < weight_total).astype(F32)
    loss = (jnp.sum((weight * stats)[:5]) - stats[5, 0]) / weight_total
    logit_grad = grad_of(logits, stats, coef, word)
    other_grad = swap_cores(logit_grad)
    grad = pull(mine, other, logit_grad, other_grad)

    one = scatter_ring(grad[:1024].reshape(4, 256, LIVE), "x")
    two = scatter_ring(grad[1024:].reshape(4, 256, LIVE), "y")
    one = scatter_direct(one.reshape(4, 64, LIVE), "y")
    two = scatter_direct(two.reshape(4, 64, LIVE), "x")
    chunk = jnp.concatenate([one.reshape(8, 8, LIVE), two.reshape(8, 8, LIVE)], 1).reshape(128, LIVE)
    spread = lax.dot_general(
        chunk, select.astype(F32), NT, precision=lax.Precision.HIGHEST, preferred_element_type=F32
    )
    spread = spread.astype(F16).reshape(8, 16, 4, 2, slots).transpose(3, 2, 0, 1, 4)
    kept = lax.dynamic_index_in_dim(spread, core, 0, keepdims=False)
    came = swap_cores(lax.dynamic_index_in_dim(spread, 1 - core, 0, keepdims=False))
    low = core == 0
    spread = jnp.stack([jnp.where(low, kept, came), jnp.where(low, came, kept)], 2)
    spread = exchange(spread.reshape(32, 32, slots), ("x", "z")).reshape(4, 8, 32, slots)
    spread = jnp.sum(spread.astype(F32), axis=1).astype(F16).reshape(128, slots)
    full = everyone(spread, ("z",)).reshape(1024, slots)
    full = place(gather_ring(full, "y"), "y").astype(F32).reshape(4, 8, 4, 2, 2, 8, slots)
    return loss, finish(full, raw, norm_gain).reshape(1, slots, width)


def solution(mesh):
    split = Mesh(mesh.devices.reshape(4, 2, 8, 4), AXES)
    return jax.shard_map(
        body,
        mesh=split,
        in_specs=(
            P(PIPE, None, None),
            P(),
            P(AXES, None),
            P(PIPE, None),
            P(PIPE, None),
            P(PIPE, None),
            P(),
            P(),
        ),
        out_specs=(P(), P(PIPE, None, None)),
        check_vma=False,
    )
```
